32 devices in a mesh: ens: 2 (over y), lon: 4 (over z), dom: 4 (over x, core).
Axes of the slice: x: 2, y: 2, z: 4, core: 2. Of those that a mesh axis runs over, the one named last changes fastest.
Arguments:
- particles: bfloat16 [16, 69, 96, 256], P(('ens', 'dom'), None, 'lon'), parts along dimension 0, may hold values from -6 to 6
- observed: bfloat16 [138, 96, 256], P('ens', 'lon'), parts along dimension 0, may hold values from -6 to 6
- precision: float32 [192, 256], P(('ens', 'lon')), parts along dimension 0, may hold values from 0.25 to 12, as said below
- stations: int32 [192, 256], P(('ens', 'lon')), parts along dimension 0, may hold values 0 or 1
- ancestors: int32 [16], P(('ens', 'dom')), parts along dimension 0, may hold values from 0 to 7
- tempering: float32 [2], P('ens'), parts along dimension 0, may hold values from 1 to 4
- w_in: bfloat16 [3, 3, 64, 69], replicated, may hold values from -0.25 to 0.25
- w_mid: bfloat16 [3, 3, 64, 64], replicated, may hold values from -0.25 to 0.25
- w_out: bfloat16 [3, 3, 69, 64], replicated, may hold values from -0.25 to 0.25
Outputs:
- new_particles: bfloat16 [16, 69, 96, 256], P(('ens', 'dom'), None, 'lon'), parts along dimension 0
- weights: float32 [16], P(('ens', 'dom')), parts along dimension 0
The draws below stay inside these ranges and needn't reach their ends.
There are 2 independent parts, one for each index of `ens`. The reference program is written for one: setup_inputs(seed, part) draws one part's arguments, and reference() takes and returns one part's arrays. A program takes and returns all parts, laid end to end along the dimension named above; an argument that names none is the same for every part. Nothing has to cross between parts.
Inputs may be any that keep to these rules, and one draw needn't show every extreme that they name: `precision`: positive everywhere; no other structure is promised. Slot s continues particle ancestors[s]; a particle may be continued by several slots or by none.
All inputs are finite; a program needn't handle non-finite values. No bound on the sum of `stations` on one device may be relied on, other than what follows from the above.
Results may differ from the reference program's by a relative error of at most 0.0021.
Values may be sent and summed in bfloat16 or wider, within the bound.
A program may use at most 128 MiB of HBM per device.

```python
import math
import jax
import jax.numpy as jnp
import numpy as np
from jax import lax

VARS = 69
HID = 64
LAT = 256
P_SIZE = 8
LON = 96


def draw_precision(key, part):
    column = jnp.arange(LON, dtype=jnp.float32)
    east_ramp = 1.0 + 2.0 * column / max(LON - 1, 1)
    rough_part = jnp.exp(jax.random.uniform(key, (LON, LAT), jnp.float32, jnp.log(0.5), jnp.log(2.0)))
    return (rough_part * east_ramp[:, None]).astype(jnp.float32)


def plant(array, own_key, low, high):
    place = [jax.random.randint(jax.random.fold_in(own_key, axis), (), 0, length) for axis, length in enumerate(array.shape)]
    longest = array.shape.index(max(array.shape))
    next_to = place[:longest] + [(place[longest] + 1) % array.shape[longest]] + place[longest + 1:]
    return array.at[tuple(place)].set(low).at[tuple(next_to)].set(high)


def block_scale(stream_key, extent, shards, smallest, top_value):
    def one(position, blocks):
        heights = jax.random.uniform(jax.random.fold_in(jax.random.fold_in(stream_key, 6), position), (blocks,), jnp.float32, smallest / len(shards), top_value / len(shards))
        return jnp.repeat(jnp.exp(heights), extent[position] // blocks).reshape((-1,) + (1,) * (len(extent) - position - 1))

    factor_of = one(*shards[0])
    for cut in shards[1:]:
        factor_of = factor_of * one(*cut)
    return factor_of


def rank_table(amount, skew):
    weights = [(1 << 20) // math.isqrt(grade ** skew) + 1 for grade in range(1, amount + 1)]
    scale = 1 + sum(weights) // (1 << 30)
    return np.cumsum(np.array([max(1, weight // scale) for weight in weights]))


def ranked(stream_key, extent, count, skew):
    table = rank_table(count, skew)
    lot = jax.random.randint(jax.random.fold_in(stream_key, 1), extent, 0, int(table[count - 1]))
    standing = jnp.searchsorted(jnp.asarray(table, jnp.int32), lot, side="right")
    return jax.random.permutation(jax.random.fold_in(stream_key, 2), count)[standing].astype(jnp.int32)


def centred(own_key, extent, width, bound, pieces=(), held_as=jnp.bfloat16):
    factor_of = block_scale(own_key, extent, pieces, -0.22, 0.18) if pieces else 1.0
    drawn = jax.random.normal(own_key, extent, jnp.float32) * width * factor_of
    return jnp.minimum(jnp.maximum(drawn, -bound), bound).astype(held_as)


def setup_inputs(seed: int = 0, part: int = 0) -> dict:
    arg_keys = jax.random.split(jax.random.key(seed), 10)
    own_keys = jax.random.split(jax.random.fold_in(arg_keys[9], part), 10)
    return {
        "particles": centred(own_keys[0], (P_SIZE, VARS, LON, LAT), 1.0, 6.0, ((0, 4), (2, 4))),
        "observed": centred(own_keys[1], (VARS, LON, LAT), 1.0, 6.0, ((1, 4),)),
        "precision": draw_precision(jax.random.fold_in(jax.random.fold_in(arg_keys[9], part), 71), part),
        "stations": plant((jax.random.randint(own_keys[3], (LON, LAT), 0, 3) < 1).astype(jnp.int32), jax.random.fold_in(own_keys[3], 1), 0, 1),
        "ancestors": plant(ranked(own_keys[4], (P_SIZE,), P_SIZE, 2), jax.random.fold_in(own_keys[4], 3), 0, P_SIZE - 1).astype(jnp.int32),
        "tempering": jnp.clip(jnp.exp(jax.random.uniform(own_keys[5], (1,), jnp.float32, math.log(1.0), math.log(4.0))), 1.0, 4.0),
        "w_in": centred(arg_keys[6], (3, 3, HID, VARS), (9 * VARS) ** -0.5, 0.25),
        "w_mid": centred(arg_keys[7], (3, 3, HID, HID), (9 * HID) ** -0.5, 0.25),
        "w_out": centred(arg_keys[8], (3, 3, VARS, HID), (9 * HID) ** -0.5, 0.25),
    }


def conv_wrap(field, weight):
    lon_cols = field.shape[1]
    lat_rows = field.shape[2]
    extended = jnp.concatenate([field[:, -1:, :], field, field[:, :1, :]], axis=1)
    extended = jnp.pad(extended, ((0, 0), (0, 0), (1, 1)))
    summed = jnp.zeros((weight.shape[2], lon_cols, lat_rows), jnp.float32)
    for row_tap in range(3):
        for col_tap in range(3):
            window = extended[:, row_tap:row_tap + lon_cols, col_tap:col_tap + lat_rows].astype(jnp.float32)
            summed = summed + jnp.einsum('oc,cxy->oxy', weight[row_tap, col_tap].astype(jnp.float32), window)
    return summed

def denoise_one(states, observed, obs_weight, w_in, w_mid, w_out):
    first_act = jax.nn.silu(conv_wrap(states, w_in)).astype(jnp.bfloat16)
    second_act = jax.nn.silu(conv_wrap(first_act, w_mid)).astype(jnp.bfloat16)
    noise_pred = conv_wrap(second_act, w_out)
    current = states.astype(jnp.float32)
    updated = current - 0.5 * noise_pred + 0.25 * obs_weight[None] * (observed.astype(jnp.float32) - current)
    return updated.astype(jnp.bfloat16)

def reference(particles, observed, precision, stations, ancestors, tempering, w_in, w_mid, w_out):
    obs_weight = stations.astype(jnp.float32) * precision
    observed_f = observed.astype(jnp.float32)

    def misfit_one(states):
        misfit_cell = states.astype(jnp.float32) - observed_f
        return jnp.sum(obs_weight[None] * misfit_cell * misfit_cell)
    misfit = lax.map(misfit_one, particles)
    center = jnp.mean(misfit)
    deviation = misfit - center
    spread = jnp.sqrt(jnp.mean(deviation * deviation) + 1.0)
    log_weights = -0.5 * tempering[0] * deviation / spread
    expo = jnp.exp(log_weights)
    weights = expo / jnp.sum(expo)
    updated = lax.map(lambda states: denoise_one(states, observed, obs_weight, w_in, w_mid, w_out), particles)
    new_particles = jnp.take(updated, ancestors.astype(jnp.int32), axis=0)
    return (new_particles, weights)
```

```python
import functools

import jax
import jax.numpy as jnp
from jax import lax
from jax.experimental import pallas as pl
from jax.experimental.pallas import tpu as pltpu
from jax.sharding import PartitionSpec as P

CHUNKS = 2
UNROLL = 2


def pad_to(count, step):
    return -(-count // step) * step


def stacked_taps(weight, out_rows, in_rows):
    _, _, outs, ins = weight.shape
    w = jnp.pad(weight, ((0, 0), (0, 0), (0, out_rows - outs), (0, in_rows - ins)))
    return w.transpose(1, 2, 0, 3).reshape(3 * out_rows, 3 * in_rows)


def conv_column(src_ref, w, x, in_rows, out_rows, first, last):
    window = src_ref[pl.ds(pl.multiple_of(x * in_rows, in_rows), 3 * in_rows), :]
    p = jnp.dot(w, window, preferred_element_type=jnp.float32)
    lat = p.shape[1]
    below = pltpu.roll(p[:out_rows], 1, 1)
    above = pltpu.roll(p[2 * out_rows :], lat - 1, 1)
    return (
        p[out_rows : 2 * out_rows]
        + jnp.where(first, 0.0, below)
        + jnp.where(last, 0.0, above)
    )


def silu(v):
    half = 0.5 * v
    return half + half * jnp.tanh(half)


def step_kernel(cols, cin, hid, nvars, ext_ref, obs_ref, ow_ref, w1_ref, w2_ref, w3_ref, out_ref, a1, a2):
    lat = out_ref.shape[-1]
    lane_h = lax.broadcasted_iota(jnp.int32, (hid, lat), 1)
    lane_o = lax.broadcasted_iota(jnp.int32, (cin, lat), 1)
    first_h, last_h = lane_h == 0, lane_h == lat - 1
    first_o, last_o = lane_o == 0, lane_o == lat - 1
    ext = ext_ref.at[0]

    def one(x, _):
        v = conv_column(ext, w1_ref[...], x, cin, hid, first_h, last_h)
        a1[pl.ds(pl.multiple_of(x * hid, hid), hid), :] = silu(v).astype(jnp.bfloat16)
        return 0

    def two(x, _):
        v = conv_column(a1, w2_ref[...], x, hid, hid, first_h, last_h)
        a2[pl.ds(pl.multiple_of(x * hid, hid), hid), :] = silu(v).astype(jnp.bfloat16)
        return 0

    def three(x, _):
        noise = conv_column(a2, w3_ref[...], x, hid, cin, first_o, last_o)
        current = ext[pl.ds(pl.multiple_of((x + 3) * cin, cin), cin), :].astype(jnp.float32)
        seen = obs_ref[x].astype(jnp.float32)
        gain = 0.25 * ow_ref[x]
        new = current - 0.5 * noise + gain * (seen - current)
        out_ref[0, x] = new[:nvars].astype(jnp.bfloat16)
        return 0

    lax.fori_loop(0, cols + 4, one, 0, unroll=UNROLL)
    lax.fori_loop(0, cols + 2, two, 0, unroll=UNROLL)
    lax.fori_loop(0, cols, three, 0, unroll=UNROLL)


def update_chunk(ext, observed, obs_weight, w1, w2, w3, nvars, hid):
    slots, wide, cin, lat = ext.shape
    cols = wide - 6
    ext = ext.reshape(slots, wide * cin, lat)
    whole = lambda a: pl.BlockSpec(a.shape, lambda p: (0,) * a.ndim)
    flops = 2 * slots * lat * ((cols + 4) * w1.size + (cols + 2) * w2.size + cols * w3.size)
    return pl.pallas_call(
        functools.partial(step_kernel, cols, cin, hid, nvars),
        out_shape=jax.ShapeDtypeStruct((slots, cols, nvars, lat), jnp.bfloat16),
        grid=(slots,),
        in_specs=[
            pl.BlockSpec((1, wide * cin, lat), lambda p: (p, 0, 0)),
            whole(observed),
            whole(obs_weight),
            whole(w1),
            whole(w2),
            whole(w3),
        ],
        out_specs=pl.BlockSpec((1, cols, nvars, lat), lambda p: (p, 0, 0, 0)),
        scratch_shapes=[
            pltpu.VMEM(((cols + 4) * hid, lat), jnp.bfloat16),
            pltpu.VMEM(((cols + 2) * hid, lat), jnp.bfloat16),
        ],
        compiler_params=pltpu.CompilerParams(vmem_limit_bytes=32 << 20),
        cost_estimate=pl.CostEstimate(
            flops=flops, bytes_accessed=2 * (ext.size + observed.size + slots * cols * nvars * lat), transcendentals=0
        ),
        name="update_chunk",
    )(ext, observed, obs_weight, w1, w2, w3)


def resample_chunk(u, own_anc, sibling_anc):
    n = lax.axis_size("dom")
    slots = u.shape[0]
    chips = n // 2
    me = lax.axis_index("dom")
    chip, core = me // 2, me % 2
    pieces = [u] + [
        lax.ppermute(u, "dom", [(d, (d + 2 * k) % n) for d in range(n)]) for k in range(1, chips)
    ]

    def pick(a):
        owner = a // slots
        value = u[0]
        for k, piece in enumerate(pieces):
            here = owner // 2 == (chip - k + chips) % chips
            for j in range(slots):
                if k or j:
                    value = jnp.where(here & (a % slots == j), piece[j], value)
        return value

    sent = jnp.stack([pick(sibling_anc[s]) for s in range(slots)])
    received = lax.ppermute(sent, "dom", [(d, d ^ 1) for d in range(n)])
    return jnp.stack(
        [
            jnp.where((own_anc[s] // slots) % 2 == core, pick(own_anc[s]), received[s])
            for s in range(slots)
        ]
    )


def on_device(particles, observed, precision, stations, ancestors, tempering, w_in, w_mid, w_out):
    slots, nvars, cols, lat = particles.shape
    hid = w_mid.shape[2]
    cin = pad_to(nvars, 16)
    n_dom, n_lon = lax.axis_size("dom"), lax.axis_size("lon")

    by_column = jnp.pad(particles.transpose(0, 2, 1, 3), ((0, 0), (0, 0), (0, cin - nvars), (0, 0)))
    ahead = [(i, (i + 1) % n_lon) for i in range(n_lon)]
    back = [(t, s) for s, t in ahead]
    low = lax.ppermute(by_column[:, cols - 3 :], "lon", ahead)
    high = lax.ppermute(by_column[:, :3], "lon", back)
    ext = jnp.concatenate([low, by_column, high], axis=1)
    sibling_anc = lax.ppermute(ancestors, "dom", [(d, d ^ 1) for d in range(n_dom)])

    obs_weight = stations.astype(jnp.float32) * precision
    misfit_cell = particles.astype(jnp.float32) - observed.astype(jnp.float32)[None]
    local_sums = jnp.sum(obs_weight[None, None] * misfit_cell * misfit_cell, axis=(1, 2, 3))
    all_sums = lax.all_gather(local_sums, ("lon", "dom"))
    every_sum = jnp.sum(all_sums.reshape(n_lon, n_dom * slots), axis=0)
    center = jnp.mean(every_sum)
    deviation = every_sum - center
    spread = jnp.sqrt(jnp.mean(deviation * deviation) + 1.0)
    log_weights = -0.5 * tempering[0] * deviation / spread
    expo = jnp.exp(log_weights)
    weights_all = expo / jnp.sum(expo)
    own_weights = lax.dynamic_slice_in_dim(weights_all, lax.axis_index("dom") * slots, slots)

    obs_columns = jnp.pad(observed.transpose(1, 0, 2), ((0, 0), (0, cin - nvars), (0, 0)))
    ow_columns = obs_weight[:, None, :]
    w1 = stacked_taps(w_in, hid, cin)
    w2 = stacked_taps(w_mid, hid, hid)
    w3 = stacked_taps(w_out, cin, hid)

    step = cols // CHUNKS
    done = []
    for c in range(CHUNKS):
        lo, hi = c * step, cols if c == CHUNKS - 1 else (c + 1) * step
        u = update_chunk(
            ext[:, lo : hi + 6], obs_columns[lo:hi], ow_columns[lo:hi], w1, w2, w3, nvars, hid
        )
        done.append(resample_chunk(u, ancestors, sibling_anc))
    new_particles = jnp.concatenate(done, axis=1).transpose(0, 2, 1, 3)
    return (new_particles, own_weights)


def solution(mesh):
    return jax.shard_map(
        on_device,
        mesh=mesh,
        in_specs=(
            P(("ens", "dom"), None, "lon", None),
            P("ens", "lon", None),
            P(("ens", "lon"), None),
            P(("ens", "lon"), None),
            P(("ens", "dom")),
            P("ens"),
            P(),
            P(),
            P(),
        ),
        out_specs=(P(("ens", "dom"), None, "lon", None), P(("ens", "dom"))),
        check_vma=False,
    )
```

```python
import functools

import jax
import jax.numpy as jnp
from jax import lax
from jax.experimental import pallas as pl
from jax.experimental.pallas import tpu as pltpu
from jax.sharding import PartitionSpec as P

CHUNKS = 3
UNROLL = True


def pad_to(count, step):
    return -(-count // step) * step


def stacked_taps(weight, out_rows, in_rows):
    _, _, outs, ins = weight.shape
    w = jnp.pad(weight, ((0, 0), (0, 0), (0, out_rows - outs), (0, in_rows - ins)))
    return w.transpose(1, 2, 0, 3).reshape(3 * out_rows, 3 * in_rows)


def conv_column(src_ref, w, x, in_rows, out_rows, first, last):
    window = src_ref[pl.ds(pl.multiple_of(x * in_rows, in_rows), 3 * in_rows), :]
    p = jnp.dot(w, window, preferred_element_type=jnp.float32)
    lat = p.shape[1]
    below = pltpu.roll(p[:out_rows], 1, 1)
    above = pltpu.roll(p[2 * out_rows :], lat - 1, 1)
    return (
        p[out_rows : 2 * out_rows]
        + jnp.where(first, 0.0, below)
        + jnp.where(last, 0.0, above)
    )


def silu(v):
    half = 0.5 * v
    return half + half * jnp.tanh(half)


def step_kernel(lo, hi, cin, hid, low_ref, mid_ref, high_ref, obs_ref, ow_ref, w1_ref, w2_ref, w3_ref, out_ref, ext, a1, a2):
    cols, nvars, lat = mid_ref.shape[1:]
    lane_h = lax.broadcasted_iota(jnp.int32, (hid, lat), 1)
    lane_o = lax.broadcasted_iota(jnp.int32, (cin, lat), 1)
    first_h, last_h = lane_h == 0, lane_h == lat - 1
    first_o, last_o = lane_o == 0, lane_o == lat - 1

    @pl.when(pl.program_id(0) == 0)
    def _():
        ext[...] = jnp.zeros_like(ext)

    for k, x in enumerate(range(lo - 3, hi + 3)):
        if x < 0:
            column = low_ref[0, x + 3]
        elif x >= cols:
            column = high_ref[0, x - cols]
        else:
            column = mid_ref[0, x]
        ext[k * cin : k * cin + nvars, :] = column

    def one(x, _):
        v = conv_column(ext, w1_ref[...], x, cin, hid, first_h, last_h)
        a1[pl.ds(pl.multiple_of(x * hid, hid), hid), :] = silu(v).astype(jnp.bfloat16)
        return 0

    def two(x, _):
        v = conv_column(a1, w2_ref[...], x, hid, hid, first_h, last_h)
        a2[pl.ds(pl.multiple_of(x * hid, hid), hid), :] = silu(v).astype(jnp.bfloat16)
        return 0

    def three(x, _):
        noise = conv_column(a2, w3_ref[...], x, hid, cin, first_o, last_o)[:nvars]
        current = ext[pl.ds(pl.multiple_of((x + 3) * cin, cin), cin), :].astype(jnp.float32)[:nvars]
        seen = obs_ref[lo + x].astype(jnp.float32)
        gain = 0.25 * ow_ref[lo + x]
        new = current - 0.5 * noise + gain * (seen - current)
        out_ref[0, x] = new.astype(jnp.bfloat16)
        return 0

    step = hi - lo
    lax.fori_loop(0, step + 4, one, 0, unroll=UNROLL)
    lax.fori_loop(0, step + 2, two, 0, unroll=UNROLL)
    lax.fori_loop(0, step, three, 0, unroll=UNROLL)


def update_chunk(lo, hi, low, mid, high, observed, obs_weight, w1, w2, w3, cin, hid):
    slots, _, nvars, lat = mid.shape
    step = hi - lo
    whole = lambda a: pl.BlockSpec(a.shape, lambda p: (0,) * a.ndim)
    own = lambda a: pl.BlockSpec((1,) + a.shape[1:], lambda p: (p, 0, 0, 0))
    flops = 2 * slots * lat * ((step + 4) * w1.size + (step + 2) * w2.size + step * w3.size)
    return pl.pallas_call(
        functools.partial(step_kernel, lo, hi, cin, hid),
        out_shape=jax.ShapeDtypeStruct((slots, step, nvars, lat), jnp.bfloat16),
        grid=(slots,),
        in_specs=[own(low), own(mid), own(high)]
        + [whole(a) for a in (observed, obs_weight, w1, w2, w3)],
        out_specs=pl.BlockSpec((1, step, nvars, lat), lambda p: (p, 0, 0, 0)),
        scratch_shapes=[
            pltpu.VMEM(((step + 6) * cin, lat), jnp.bfloat16),
            pltpu.VMEM(((step + 4) * hid, lat), jnp.bfloat16),
            pltpu.VMEM(((step + 2) * hid, lat), jnp.bfloat16),
        ],
        compiler_params=pltpu.CompilerParams(vmem_limit_bytes=24 << 20),
        cost_estimate=pl.CostEstimate(
            flops=flops * 8, bytes_accessed=2 * (mid.size + observed.size + slots * step * nvars * lat), transcendentals=0
        ),
        name="update_chunk",
    )(low, mid, high, observed, obs_weight, w1, w2, w3)


def exchange_kernel(n_lon, n_dom, mid_ref, sums_ref, low_ref, high_ref, all_ref, parts, total, edge_send, edge_recv, lon_send, lon_recv, dom_send, dom_recv):
    lon, dom = lax.axis_index("lon"), lax.axis_index("dom")
    cols = mid_ref.shape[1]

    def lon_at(k):
        return {"lon": lax.rem(lon + k, n_lon)}

    def dom_at(k):
        return {"dom": lax.rem(dom + k, n_dom)}

    barrier = pltpu.get_barrier_semaphore()
    for k in range(1, n_lon):
        pl.semaphore_signal(barrier, inc=1, device_id=lon_at(k), device_id_type=pl.DeviceIdType.MESH)
    for k in range(1, n_dom):
        pl.semaphore_signal(barrier, inc=1, device_id=dom_at(k), device_id_type=pl.DeviceIdType.MESH)
    pl.semaphore_wait(barrier, n_lon + n_dom - 2)

    def send(src, dst, s, r, target):
        copy = pltpu.make_async_remote_copy(
            src_ref=src, dst_ref=dst, send_sem=s, recv_sem=r,
            device_id=target, device_id_type=pl.DeviceIdType.MESH,
        )
        copy.start()
        return copy

    edges = [
        send(mid_ref.at[:, cols - 3 : cols], low_ref, edge_send.at[0], edge_recv.at[0], lon_at(1)),
        send(mid_ref.at[:, 0:3], high_ref, edge_send.at[1], edge_recv.at[1], lon_at(n_lon - 1)),
    ]
    parts[lon] = sums_ref[...]
    over_lon = [
        send(sums_ref, parts.at[lon], lon_send.at[k - 1], lon_recv.at[k - 1], lon_at(k))
        for k in range(1, n_lon)
    ]
    for copy in over_lon:
        copy.wait()
    band_sum = parts[0]
    for k in range(1, n_lon):
        band_sum = band_sum + parts[k]
    total[...] = band_sum
    all_ref[dom] = band_sum
    over_dom = [
        send(total, all_ref.at[dom], dom_send.at[k - 1], dom_recv.at[k - 1], dom_at(k))
        for k in range(1, n_dom)
    ]
    for copy in over_dom + edges:
        copy.wait()


def exchange(mid, sums, n_lon, n_dom):
    slots, _, nvars, lat = mid.shape
    edge = jax.ShapeDtypeStruct((slots, 3, nvars, lat), mid.dtype)
    vmem = pl.BlockSpec(memory_space=pltpu.VMEM)
    return pl.pallas_call(
        functools.partial(exchange_kernel, n_lon, n_dom),
        out_shape=(edge, edge, jax.ShapeDtypeStruct((n_dom,) + sums.shape, jnp.float32)),
        in_specs=[pl.BlockSpec(memory_space=pl.ANY), vmem],
        out_specs=(vmem, vmem, vmem),
        scratch_shapes=[
            pltpu.VMEM((n_lon,) + sums.shape, jnp.float32),
            pltpu.VMEM(sums.shape, jnp.float32),
            pltpu.SemaphoreType.DMA((2,)),
            pltpu.SemaphoreType.DMA((2,)),
            pltpu.SemaphoreType.DMA((n_lon - 1,)),
            pltpu.SemaphoreType.DMA((n_lon - 1,)),
            pltpu.SemaphoreType.DMA((n_dom - 1,)),
            pltpu.SemaphoreType.DMA((n_dom - 1,)),
        ],
        compiler_params=pltpu.CompilerParams(collective_id=0, has_side_effects=True),
        name="exchange",
    )(mid, sums)


def resample_chunk(u, candidate, here):
    n = lax.axis_size("dom")
    slots = u.shape[0]
    pieces = [u] + [
        lax.ppermute(u, "dom", [(d, (d + 2 * k) % n) for d in range(n)]) for k in range(1, n // 2)
    ]

    def pick(c):
        value = u[0]
        for m in range(1, len(pieces) * slots):
            value = jnp.where(c == m, pieces[m // slots][m % slots], value)
        return value

    sent = jnp.stack([pick(candidate[slots + s]) for s in range(slots)])
    received = lax.ppermute(sent, "dom", [(d, d ^ 1) for d in range(n)])
    return jnp.stack([jnp.where(here[s], pick(candidate[s]), received[s]) for s in range(slots)])


def on_device(particles, observed, precision, stations, ancestors, tempering, w_in, w_mid, w_out):
    slots, nvars, cols, lat = particles.shape
    hid = w_mid.shape[2]
    cin = pad_to(nvars, 16)
    n_dom, n_lon = lax.axis_size("dom"), lax.axis_size("lon")
    me = lax.axis_index("dom")
    mid = particles.transpose(0, 2, 1, 3)
    sibling_anc = lax.ppermute(ancestors, "dom", [(d, d ^ 1) for d in range(n_dom)])

    obs_weight = stations.astype(jnp.float32) * precision
    misfit_cell = particles.astype(jnp.float32) - observed.astype(jnp.float32)[None]
    local_sums = jnp.sum(obs_weight[None, None] * misfit_cell * misfit_cell, axis=(1, 2))
    sums = jnp.sum(local_sums.reshape(slots, lat // 128, 128), axis=1)
    sums = jnp.pad(sums, ((0, pad_to(slots, 8) - slots), (0, 0)))
    low, high, all_sums = exchange(mid, sums, n_lon, n_dom)
    every_sum = jnp.sum(all_sums[:, :slots], axis=2).reshape(n_dom * slots)
    center = jnp.mean(every_sum)
    deviation = every_sum - center
    spread = jnp.sqrt(jnp.mean(deviation * deviation) + 1.0)
    log_weights = -0.5 * tempering[0] * deviation / spread
    expo = jnp.exp(log_weights)
    weights_all = expo / jnp.sum(expo)
    own_weights = lax.dynamic_slice_in_dim(weights_all, me * slots, slots)

    wanted = jnp.concatenate([ancestors, sibling_anc])
    owner = lax.div(wanted, slots)
    chips = n_dom // 2
    steps = lax.rem(lax.shift_right_logical(me, 1) - lax.div(owner, 2) + chips, chips)
    candidate = steps * slots + lax.rem(wanted, slots)
    here = lax.rem(owner, 2) == (me & 1)

    obs_columns = observed.transpose(1, 0, 2)
    ow_columns = obs_weight[:, None, :]
    w1 = stacked_taps(w_in, hid, cin)
    w2 = stacked_taps(w_mid, hid, hid)
    w3 = stacked_taps(w_out, cin, hid)

    bounds = [cols * c // CHUNKS for c in range(CHUNKS + 1)]
    done = []
    for lo, hi in zip(bounds, bounds[1:]):
        u = update_chunk(lo, hi, low, mid, high, obs_columns, ow_columns, w1, w2, w3, cin, hid)
        done.append(resample_chunk(u, candidate, here))
    new_particles = jnp.concatenate(done, axis=1).transpose(0, 2, 1, 3)
    return (new_particles, own_weights)


def solution(mesh):
    return jax.shard_map(
        on_device,
        mesh=mesh,
        in_specs=(
            P(("ens", "dom"), None, "lon", None),
            P("ens", "lon", None),
            P(("ens", "lon"), None),
            P(("ens", "lon"), None),
            P(("ens", "dom")),
            P("ens"),
            P(),
            P(),
            P(),
        ),
        out_specs=(P(("ens", "dom"), None, "lon", None), P(("ens", "dom"))),
        check_vma=False,
    )
```

```python
import functools

import jax
import jax.numpy as jnp
from jax import lax
from jax.experimental import pallas as pl
from jax.experimental.pallas import tpu as pltpu
from jax.sharding import PartitionSpec as P


def pad_to(count, step):
    return -(-count // step) * step


def stacked_taps(weight, out_rows, in_rows):
    _, _, outs, ins = weight.shape
    w = jnp.pad(weight, ((0, 0), (0, 0), (0, out_rows - outs), (0, in_rows - ins)))
    return w.transpose(1, 2, 0, 3).reshape(3 * out_rows, 3 * in_rows)


def conv_column(src_ref, w, x, in_rows, out_rows, first, last):
    window = src_ref[x * in_rows : (x + 3) * in_rows, :]
    p = jnp.dot(w, window, preferred_element_type=jnp.float32)
    lat = p.shape[1]
    below = pltpu.roll(p[:out_rows], 1, 1)
    above = pltpu.roll(p[2 * out_rows :], lat - 1, 1)
    return (
        p[out_rows : 2 * out_rows]
        + jnp.where(first, 0.0, below)
        + jnp.where(last, 0.0, above)
    )


def silu(v):
    half = 0.5 * v
    return half + half * jnp.tanh(half)


def step_kernel(spans, cin, hid, edges, *refs):
    if edges:
        low_ref, high_ref, *refs = refs
    mid_ref, obs_ref, ow_ref, w1_ref, w2_ref, w3_ref, out_ref, ext, a1, a2 = refs
    cols, nvars, lat = mid_ref.shape[1:]
    lane_h = lax.broadcasted_iota(jnp.int32, (hid, lat), 1)
    lane_o = lax.broadcasted_iota(jnp.int32, (cin, lat), 1)
    first_h, last_h = lane_h == 0, lane_h == lat - 1
    first_o, last_o = lane_o == 0, lane_o == lat - 1

    @pl.when(pl.program_id(0) == 0)
    def _():
        ext[...] = jnp.zeros_like(ext)

    at = 0
    for s, (lo, hi) in enumerate(spans):
        for k, x in enumerate(range(lo - 3, hi + 3)):
            if x < 0:
                column = low_ref[0, x + 3]
            elif x >= cols:
                column = high_ref[0, x - cols]
            else:
                column = mid_ref[0, x]
            ext[s, k * cin : k * cin + nvars, :] = column
        for x in range(hi - lo + 4):
            v = conv_column(ext.at[s], w1_ref[...], x, cin, hid, first_h, last_h)
            a1[s, x * hid : (x + 1) * hid, :] = silu(v).astype(jnp.bfloat16)
        for x in range(hi - lo + 2):
            v = conv_column(a1.at[s], w2_ref[...], x, hid, hid, first_h, last_h)
            a2[s, x * hid : (x + 1) * hid, :] = silu(v).astype(jnp.bfloat16)
        for x in range(hi - lo):
            noise = conv_column(a2.at[s], w3_ref[...], x, hid, cin, first_o, last_o)[:nvars]
            current = ext[s, (x + 3) * cin : (x + 4) * cin, :].astype(jnp.float32)[:nvars]
            seen = obs_ref[lo + x].astype(jnp.float32)
            gain = 0.25 * ow_ref[lo + x]
            new = current - 0.5 * noise + gain * (seen - current)
            out_ref[0, at] = new.astype(jnp.bfloat16)
            at += 1


def update_chunk(spans, edges, mid, observed, obs_weight, w1, w2, w3, cin, hid):
    slots, _, nvars, lat = mid.shape
    step = sum(hi - lo for lo, hi in spans)
    widest = max(hi - lo for lo, hi in spans)
    whole = lambda a: pl.BlockSpec(a.shape, lambda p: (0,) * a.ndim)
    own = lambda a: pl.BlockSpec((1,) + a.shape[1:], lambda p: (p, 0, 0, 0))
    return pl.pallas_call(
        functools.partial(step_kernel, spans, cin, hid, bool(edges)),
        out_shape=jax.ShapeDtypeStruct((slots, step, nvars, lat), jnp.bfloat16),
        grid=(slots,),
        in_specs=[own(a) for a in (*edges, mid)]
        + [whole(a) for a in (observed, obs_weight, w1, w2, w3)],
        out_specs=pl.BlockSpec((1, step, nvars, lat), lambda p: (p, 0, 0, 0)),
        scratch_shapes=[
            pltpu.VMEM((len(spans), (widest + 6) * cin, lat), jnp.bfloat16),
            pltpu.VMEM((len(spans), (widest + 4) * hid, lat), jnp.bfloat16),
            pltpu.VMEM((len(spans), (widest + 2) * hid, lat), jnp.bfloat16),
        ],
        compiler_params=pltpu.CompilerParams(vmem_limit_bytes=24 << 20),
        cost_estimate=pl.CostEstimate(flops=0, bytes_accessed=1024, transcendentals=0),
        name="update_chunk",
    )(*edges, mid, observed, obs_weight, w1, w2, w3)


def exchange_kernel(n_lon, mid_ref, sums_ref, low_ref, high_ref, total_ref, parts, edge_send, edge_recv, lon_send, lon_recv):
    lon = lax.axis_index("lon")
    cols = mid_ref.shape[1]

    def lon_at(k):
        return {"lon": lax.rem(lon + k, n_lon)}

    barrier = pltpu.get_barrier_semaphore()
    for k in range(1, n_lon):
        pl.semaphore_signal(barrier, inc=1, device_id=lon_at(k), device_id_type=pl.DeviceIdType.MESH)
    pl.semaphore_wait(barrier, n_lon - 1)

    def send(src, dst, s, r, target):
        copy = pltpu.make_async_remote_copy(
            src_ref=src, dst_ref=dst, send_sem=s, recv_sem=r,
            device_id=target, device_id_type=pl.DeviceIdType.MESH,
        )
        copy.start()
        return copy

    edges = [
        send(mid_ref.at[:, cols - 3 : cols], low_ref, edge_send.at[0], edge_recv.at[0], lon_at(1)),
        send(mid_ref.at[:, 0:3], high_ref, edge_send.at[1], edge_recv.at[1], lon_at(n_lon - 1)),
    ]
    parts[lon] = sums_ref[...]
    over_lon = [
        send(sums_ref, parts.at[lon], lon_send.at[k - 1], lon_recv.at[k - 1], lon_at(k))
        for k in range(1, n_lon)
    ]
    for copy in over_lon:
        copy.wait()
    band_sum = parts[0]
    for k in range(1, n_lon):
        band_sum = band_sum + parts[k]
    total_ref[...] = band_sum
    for copy in edges:
        copy.wait()


def exchange(mid, sums, n_lon):
    slots, _, nvars, lat = mid.shape
    edge = jax.ShapeDtypeStruct((slots, 3, nvars, lat), mid.dtype)
    vmem = pl.BlockSpec(memory_space=pltpu.VMEM)
    return pl.pallas_call(
        functools.partial(exchange_kernel, n_lon),
        out_shape=(edge, edge, jax.ShapeDtypeStruct(sums.shape, jnp.float32)),
        in_specs=[pl.BlockSpec(memory_space=pl.ANY), vmem],
        out_specs=(vmem, vmem, vmem),
        scratch_shapes=[
            pltpu.VMEM((n_lon,) + sums.shape, jnp.float32),
            pltpu.SemaphoreType.DMA((2,)),
            pltpu.SemaphoreType.DMA((2,)),
            pltpu.SemaphoreType.DMA((n_lon - 1,)),
            pltpu.SemaphoreType.DMA((n_lon - 1,)),
        ],
        compiler_params=pltpu.CompilerParams(collective_id=0, has_side_effects=True),
        cost_estimate=pl.CostEstimate(flops=0, bytes_accessed=1024, transcendentals=0),
        name="exchange",
    )(mid, sums)


def across(u):
    n = lax.axis_size("dom")
    return [u] + [
        lax.ppermute(u, "dom", [(d, (d + 2 * k) % n) for d in range(n)]) for k in range(1, n // 2)
    ]


def pick(pieces, c):
    slots = pieces[0].shape[0]
    value = pieces[0][0]
    for m in range(1, len(pieces) * slots):
        value = jnp.where(c == m, pieces[m // slots][m % slots], value)
    return value


def on_device(particles, observed, precision, stations, ancestors, tempering, w_in, w_mid, w_out):
    slots, nvars, cols, lat = particles.shape
    hid = w_mid.shape[2]
    cin = pad_to(nvars, 16)
    n_dom, n_lon = lax.axis_size("dom"), lax.axis_size("lon")
    me = lax.axis_index("dom")
    mid = particles.transpose(0, 2, 1, 3)
    sibling_anc = lax.ppermute(ancestors, "dom", [(d, d ^ 1) for d in range(n_dom)])

    obs_weight = stations.astype(jnp.float32) * precision
    wanted = jnp.concatenate([ancestors, sibling_anc])
    owner = lax.div(wanted, slots)
    chips = n_dom // 2
    steps = lax.rem(lax.shift_right_logical(me, 1) - lax.div(owner, 2) + chips, chips)
    candidate = steps * slots + lax.rem(wanted, slots)
    here = lax.rem(owner, 2) == (me & 1)

    obs_columns = observed.transpose(1, 0, 2)
    ow_columns = obs_weight[:, None, :]
    w1 = stacked_taps(w_in, hid, cin)
    w2 = stacked_taps(w_mid, hid, hid)
    w3 = stacked_taps(w_out, cin, hid)

    update = lambda spans, edges: update_chunk(
        spans, edges, mid, obs_columns, ow_columns, w1, w2, w3, cin, hid
    )
    u = update([(3, cols - 3)], [])
    groups = [across(u)]

    late_weight, _ = lax.optimization_barrier((obs_weight, u))
    misfit_cell = particles.astype(jnp.float32) - observed.astype(jnp.float32)[None]
    local_sums = jnp.sum(late_weight[None, None] * misfit_cell * misfit_cell, axis=(1, 2))
    sums = jnp.sum(local_sums.reshape(slots, lat // 128, 128), axis=1)
    sums = jnp.pad(sums, ((0, pad_to(slots, 8) - slots), (0, 0)))
    low, high, band_sums = exchange(mid, sums, n_lon)
    groups.append(across(update([(0, 3), (cols - 3, cols)], [low, high])))

    own_misfit = jnp.sum(band_sums[:slots], axis=1)
    every_sum = jnp.concatenate(
        [own_misfit]
        + [
            lax.ppermute(own_misfit, "dom", [(d, (d + k) % n_dom) for d in range(n_dom)])
            for k in range(1, n_dom)
        ]
    )
    center = jnp.mean(every_sum)
    deviation = every_sum - center
    spread = jnp.sqrt(jnp.mean(deviation * deviation) + 1.0)
    expo = jnp.exp(-0.5 * tempering[0] * deviation / spread)
    own_weights = expo[:slots] / jnp.sum(expo)

    done, before = [], None
    for pieces in groups:
        if before is not None:
            *pieces, before = lax.optimization_barrier((*pieces, before))
            done[-1] = before
        sent = jnp.stack([pick(pieces, candidate[slots + s]) for s in range(slots)])
        before = sent
        done.append(sent)
        groups[len(done) - 1] = pieces
    results = []
    for pieces, sent in zip(groups, done):
        received = lax.ppermute(sent, "dom", [(d, d ^ 1) for d in range(n_dom)])
        results.append(
            jnp.stack([jnp.where(here[s], pick(pieces, candidate[s]), received[s]) for s in range(slots)])
        )
    inner, sides = results
    new_columns = jnp.concatenate([sides[:, :3], inner, sides[:, 3:]], axis=1)
    return (new_columns.transpose(0, 2, 1, 3), own_weights)


def solution(mesh):
    return jax.shard_map(
        on_device,
        mesh=mesh,
        in_specs=(
            P(("ens", "dom"), None, "lon", None),
            P("ens", "lon", None),
            P(("ens", "lon"), None),
            P(("ens", "lon"), None),
            P(("ens", "dom")),
            P("ens"),
            P(),
            P(),
            P(),
        ),
        out_specs=(P(("ens", "dom"), None, "lon", None), P(("ens", "dom"))),
        check_vma=False,
    )
```

```python
import functools

import jax
import jax.numpy as jnp
from jax import lax
from jax.experimental import pallas as pl
from jax.experimental.pallas import tpu as pltpu
from jax.sharding import PartitionSpec as P


def pad_to(count, step):
    return -(-count // step) * step


def stacked_taps(weight, out_rows, in_rows):
    _, _, outs, ins = weight.shape
    w = jnp.pad(weight, ((0, 0), (0, 0), (0, out_rows - outs), (0, in_rows - ins)))
    return w.transpose(1, 2, 0, 3).reshape(3 * out_rows, 3 * in_rows)


def conv_column(src_ref, w, x, in_rows, out_rows, first, last):
    window = src_ref[x * in_rows : (x + 3) * in_rows, :]
    p = jnp.dot(w, window, preferred_element_type=jnp.float32)
    lat = p.shape[1]
    below = pltpu.roll(p[:out_rows], 1, 1)
    above = pltpu.roll(p[2 * out_rows :], lat - 1, 1)
    return (
        p[out_rows : 2 * out_rows]
        + jnp.where(first, 0.0, below)
        + jnp.where(last, 0.0, above)
    )


def silu(v):
    half = 0.5 * v
    return half + half * jnp.tanh(half)


def step_kernel(spans, cin, hid, edges, *refs):
    if edges:
        low_ref, high_ref, *refs = refs
    mid_ref, obs_ref, ow_ref, w1_ref, w2_ref, w3_ref, out_ref, ext, a1, a2 = refs
    cols, nvars, lat = mid_ref.shape[1:]
    lane_h = lax.broadcasted_iota(jnp.int32, (hid, lat), 1)
    lane_o = lax.broadcasted_iota(jnp.int32, (cin, lat), 1)
    first_h, last_h = lane_h == 0, lane_h == lat - 1
    first_o, last_o = lane_o == 0, lane_o == lat - 1

    @pl.when(pl.program_id(0) == 0)
    def _():
        ext[...] = jnp.zeros_like(ext)

    at = 0
    for s, (lo, hi) in enumerate(spans):
        for k, x in enumerate(range(lo - 3, hi + 3)):
            if x < 0:
                column = low_ref[0, x + 3]
            elif x >= cols:
                column = high_ref[0, x - cols]
            else:
                column = mid_ref[0, x]
            ext[s, k * cin : k * cin + nvars, :] = column
        for x in range(hi - lo + 4):
            v = conv_column(ext.at[s], w1_ref[...], x, cin, hid, first_h, last_h)
            a1[s, x * hid : (x + 1) * hid, :] = silu(v).astype(jnp.bfloat16)
        for x in range(hi - lo + 2):
            v = conv_column(a1.at[s], w2_ref[...], x, hid, hid, first_h, last_h)
            a2[s, x * hid : (x + 1) * hid, :] = silu(v).astype(jnp.bfloat16)
        for x in range(hi - lo):
            noise = conv_column(a2.at[s], w3_ref[...], x, hid, cin, first_o, last_o)[:nvars]
            current = ext[s, (x + 3) * cin : (x + 4) * cin, :].astype(jnp.float32)[:nvars]
            seen = obs_ref[lo + x].astype(jnp.float32)
            gain = 0.25 * ow_ref[lo + x]
            new = current - 0.5 * noise + gain * (seen - current)
            out_ref[0, at] = new.astype(jnp.bfloat16)
            at += 1


def update_chunk(spans, edges, mid, observed, obs_weight, w1, w2, w3, cin, hid):
    slots, _, nvars, lat = mid.shape
    step = sum(hi - lo for lo, hi in spans)
    widest = max(hi - lo for lo, hi in spans)
    whole = lambda a: pl.BlockSpec(a.shape, lambda p: (0,) * a.ndim)
    own = lambda a: pl.BlockSpec((1,) + a.shape[1:], lambda p: (p, 0, 0, 0))
    return pl.pallas_call(
        functools.partial(step_kernel, spans, cin, hid, bool(edges)),
        out_shape=jax.ShapeDtypeStruct((slots, step, nvars, lat), jnp.bfloat16),
        grid=(slots,),
        in_specs=[own(a) for a in (*edges, mid)]
        + [whole(a) for a in (observed, obs_weight, w1, w2, w3)],
        out_specs=pl.BlockSpec((1, step, nvars, lat), lambda p: (p, 0, 0, 0)),
        scratch_shapes=[
            pltpu.VMEM((len(spans), (widest + 6) * cin, lat), jnp.bfloat16),
            pltpu.VMEM((len(spans), (widest + 4) * hid, lat), jnp.bfloat16),
            pltpu.VMEM((len(spans), (widest + 2) * hid, lat), jnp.bfloat16),
        ],
        compiler_params=pltpu.CompilerParams(vmem_limit_bytes=56 << 20),
        cost_estimate=pl.CostEstimate(flops=0, bytes_accessed=1024, transcendentals=0),
        name="update_chunk",
    )(*edges, mid, observed, obs_weight, w1, w2, w3)


def exchange_kernel(n_lon, mid_ref, sums_ref, low_ref, high_ref, total_ref, parts, edge_send, edge_recv, lon_send, lon_recv):
    lon = lax.axis_index("lon")
    cols = mid_ref.shape[1]

    def lon_at(k):
        return {"lon": lax.rem(lon + k, n_lon)}

    barrier = pltpu.get_barrier_semaphore()
    for k in range(1, n_lon):
        pl.semaphore_signal(barrier, inc=1, device_id=lon_at(k), device_id_type=pl.DeviceIdType.MESH)
    pl.semaphore_wait(barrier, n_lon - 1)

    def send(src, dst, s, r, target):
        copy = pltpu.make_async_remote_copy(
            src_ref=src, dst_ref=dst, send_sem=s, recv_sem=r,
            device_id=target, device_id_type=pl.DeviceIdType.MESH,
        )
        copy.start()
        return copy

    edges = [
        send(mid_ref.at[:, cols - 3 : cols], low_ref, edge_send.at[0], edge_recv.at[0], lon_at(1)),
        send(mid_ref.at[:, 0:3], high_ref, edge_send.at[1], edge_recv.at[1], lon_at(n_lon - 1)),
    ]
    parts[lon] = sums_ref[...]
    over_lon = [
        send(sums_ref, parts.at[lon], lon_send.at[k - 1], lon_recv.at[k - 1], lon_at(k))
        for k in range(1, n_lon)
    ]
    for copy in over_lon:
        copy.wait()
    band_sum = parts[0]
    for k in range(1, n_lon):
        band_sum = band_sum + parts[k]
    total_ref[...] = band_sum
    for copy in edges:
        copy.wait()


def exchange(mid, sums, n_lon):
    slots, _, nvars, lat = mid.shape
    edge = jax.ShapeDtypeStruct((slots, 3, nvars, lat), mid.dtype)
    vmem = pl.BlockSpec(memory_space=pltpu.VMEM)
    return pl.pallas_call(
        functools.partial(exchange_kernel, n_lon),
        out_shape=(edge, edge, jax.ShapeDtypeStruct(sums.shape, jnp.float32)),
        in_specs=[pl.BlockSpec(memory_space=pl.ANY), vmem],
        out_specs=(vmem, vmem, vmem),
        scratch_shapes=[
            pltpu.VMEM((n_lon,) + sums.shape, jnp.float32),
            pltpu.SemaphoreType.DMA((2,)),
            pltpu.SemaphoreType.DMA((2,)),
            pltpu.SemaphoreType.DMA((n_lon - 1,)),
            pltpu.SemaphoreType.DMA((n_lon - 1,)),
        ],
        compiler_params=pltpu.CompilerParams(collective_id=0, has_side_effects=True),
        cost_estimate=pl.CostEstimate(flops=0, bytes_accessed=1024, transcendentals=0),
        name="exchange",
    )(mid, sums)


def across(u):
    n = lax.axis_size("dom")
    return [u] + [
        lax.ppermute(u, "dom", [(d, (d + 2 * k) % n) for d in range(n)]) for k in range(1, n // 2)
    ]


def pick_kernel(slots, base, codes_ref, *refs):
    *pieces, out_ref = refs
    if base == 0:
        received_ref, *pieces = pieces
    for s in range(slots):
        for m in range(len(pieces) * slots):
            wanted = codes_ref[base + s] == m
            if base == 0:
                wanted = wanted & (codes_ref[2 * slots + s] == 1)

            @pl.when(wanted)
            def _():
                out_ref[s] = pieces[m // slots][m % slots]

        if base == 0:

            @pl.when(codes_ref[2 * slots + s] == 0)
            def _():
                out_ref[s] = received_ref[s]


def pick(codes, base, arrays):
    u = arrays[0]
    slots = u.shape[0]
    vmem = pl.BlockSpec(memory_space=pltpu.VMEM)
    return pl.pallas_call(
        functools.partial(pick_kernel, slots, base),
        out_shape=jax.ShapeDtypeStruct(u.shape, u.dtype),
        in_specs=[pl.BlockSpec(memory_space=pltpu.SMEM)] + [vmem] * len(arrays),
        out_specs=vmem,
        compiler_params=pltpu.CompilerParams(vmem_limit_bytes=24 << 20),
        cost_estimate=pl.CostEstimate(flops=0, bytes_accessed=1024, transcendentals=0),
        name="pick",
    )(codes, *arrays)


def weight_kernel(slots, t_ref, *refs):
    *part_refs, out_ref = refs
    shape = out_ref.shape
    real = lax.broadcasted_iota(jnp.int32, shape, 0) < slots
    count = len(part_refs) * slots

    def over_particles(rows):
        total = rows[0]
        for row in rows[1:]:
            total = total + row
        return jnp.sum(total, axis=0, keepdims=True)

    misfits = [jnp.broadcast_to(jnp.sum(r[...], axis=1, keepdims=True), shape) for r in part_refs]
    center = over_particles([jnp.where(real, m, 0.0) for m in misfits]) / count
    deviations = [jnp.where(real, m - center, 0.0) for m in misfits]
    spread = jnp.sqrt(over_particles([d * d for d in deviations]) / count + 1.0)
    expos = [jnp.where(real, jnp.exp(-0.5 * t_ref[0] * d / spread), 0.0) for d in deviations]
    out_ref[...] = expos[0] / over_particles(expos)


def own_weights_of(parts, tempering, slots):
    vmem = pl.BlockSpec(memory_space=pltpu.VMEM)
    out = pl.pallas_call(
        functools.partial(weight_kernel, slots),
        out_shape=jax.ShapeDtypeStruct(parts[0].shape, jnp.float32),
        in_specs=[pl.BlockSpec(memory_space=pltpu.SMEM)] + [vmem] * len(parts),
        out_specs=vmem,
        name="own_weights",
    )(tempering, *parts)
    return out[:slots, 0]


def on_device(particles, observed, precision, stations, ancestors, tempering, w_in, w_mid, w_out):
    slots, nvars, cols, lat = particles.shape
    hid = w_mid.shape[2]
    cin = pad_to(nvars, 16)
    n_dom, n_lon = lax.axis_size("dom"), lax.axis_size("lon")
    me = lax.axis_index("dom")
    mid = particles.transpose(0, 2, 1, 3)
    sibling_anc = lax.ppermute(ancestors, "dom", [(d, d ^ 1) for d in range(n_dom)])

    obs_weight = stations.astype(jnp.float32) * precision
    wanted = jnp.concatenate([ancestors, sibling_anc])
    owner = lax.div(wanted, slots)
    chips = n_dom // 2
    steps = lax.rem(lax.shift_right_logical(me, 1) - lax.div(owner, 2) + chips, chips)
    candidate = steps * slots + lax.rem(wanted, slots)
    here = lax.rem(owner, 2) == (me & 1)

    obs_columns = observed.transpose(1, 0, 2)
    ow_columns = obs_weight[:, None, :]
    w1 = stacked_taps(w_in, hid, cin)
    w2 = stacked_taps(w_mid, hid, hid)
    w3 = stacked_taps(w_out, cin, hid)

    update = lambda spans, edges: update_chunk(
        spans, edges, mid, obs_columns, ow_columns, w1, w2, w3, cin, hid
    )
    u = update([(3, cols - 3)], [])
    groups = [across(u)]

    late_weight, _ = lax.optimization_barrier((obs_weight, u))
    misfit_cell = particles.astype(jnp.float32) - observed.astype(jnp.float32)[None]
    local_sums = jnp.sum(late_weight[None, None] * misfit_cell * misfit_cell, axis=(1, 2))
    sums = jnp.sum(local_sums.reshape(slots, lat // 128, 128), axis=1)
    sums = jnp.pad(sums, ((0, pad_to(slots, 8) - slots), (0, 0)))
    low, high, band_sums = exchange(mid, sums, n_lon)
    groups.append(across(update([(0, 3), (cols - 3, cols)], [low, high])))

    parts = [band_sums] + [
        lax.ppermute(band_sums, "dom", [(d, (d + k) % n_dom) for d in range(n_dom)])
        for k in range(1, n_dom)
    ]
    own_weights = own_weights_of(parts, tempering, slots)

    codes = jnp.concatenate([candidate, here[:slots].astype(jnp.int32)])
    codes, _ = lax.optimization_barrier((codes, groups[-1][0]))
    results, before = [], None
    for pieces in groups:
        if before is not None:
            *pieces, before = lax.optimization_barrier((*pieces, before))
        sent = pick(codes, slots, pieces)
        before = sent
        received = lax.ppermute(sent, "dom", [(d, d ^ 1) for d in range(n_dom)])
        results.append(pick(codes, 0, [received, *pieces]))
    inner, sides = results
    new_columns = jnp.concatenate([sides[:, :3], inner, sides[:, 3:]], axis=1)
    return (new_columns.transpose(0, 2, 1, 3), own_weights)


def solution(mesh):
    return jax.shard_map(
        on_device,
        mesh=mesh,
        in_specs=(
            P(("ens", "dom"), None, "lon", None),
            P("ens", "lon", None),
            P(("ens", "lon"), None),
            P(("ens", "lon"), None),
            P(("ens", "dom")),
            P("ens"),
            P(),
            P(),
            P(),
        ),
        out_specs=(P(("ens", "dom"), None, "lon", None), P(("ens", "dom"))),
        check_vma=False,
    )
```

```python
import functools

import jax
import jax.numpy as jnp
from jax import lax
from jax.experimental import pallas as pl
from jax.experimental.pallas import tpu as pltpu
from jax.sharding import PartitionSpec as P


def pad_to(count, step):
    return -(-count // step) * step


def stacked_taps(weight, out_rows, in_rows):
    _, _, outs, ins = weight.shape
    w = jnp.pad(weight, ((0, 0), (0, 0), (0, out_rows - outs), (0, in_rows - ins)))
    return w.transpose(1, 2, 0, 3).reshape(3 * out_rows, 3 * in_rows)


def conv_column(src_ref, w, x, in_rows, out_rows, first, last):
    window = src_ref[x * in_rows : (x + 3) * in_rows, :]
    p = jnp.dot(w, window, preferred_element_type=jnp.float32)
    lat = p.shape[1]
    below = pltpu.roll(p[:out_rows], 1, 1)
    above = pltpu.roll(p[2 * out_rows :], lat - 1, 1)
    return (
        p[out_rows : 2 * out_rows]
        + jnp.where(first, 0.0, below)
        + jnp.where(last, 0.0, above)
    )


def silu(v):
    half = 0.5 * v
    return half + half * jnp.tanh(half)


def step_kernel(spans, cin, hid, edges, *refs):
    if edges:
        low_ref, high_ref, *refs = refs
    mid_ref, obs_ref, ow_ref, w1_ref, w2_ref, w3_ref, out_ref, ext, a1, a2 = refs
    cols, nvars, lat = mid_ref.shape[1:]
    lane_h = lax.broadcasted_iota(jnp.int32, (hid, lat), 1)
    lane_o = lax.broadcasted_iota(jnp.int32, (cin, lat), 1)
    first_h, last_h = lane_h == 0, lane_h == lat - 1
    first_o, last_o = lane_o == 0, lane_o == lat - 1

    @pl.when(pl.program_id(0) == 0)
    def _():
        ext[...] = jnp.zeros_like(ext)

    at = 0
    for s, (lo, hi) in enumerate(spans):
        for k, x in enumerate(range(lo - 3, hi + 3)):
            if x < 0:
                column = low_ref[0, x + 3]
            elif x >= cols:
                column = high_ref[0, x - cols]
            else:
                column = mid_ref[0, x]
            ext[s, k * cin : k * cin + nvars, :] = column
        for x in range(hi - lo + 4):
            v = conv_column(ext.at[s], w1_ref[...], x, cin, hid, first_h, last_h)
            a1[s, x * hid : (x + 1) * hid, :] = silu(v).astype(jnp.bfloat16)
        for x in range(hi - lo + 2):
            v = conv_column(a1.at[s], w2_ref[...], x, hid, hid, first_h, last_h)
            a2[s, x * hid : (x + 1) * hid, :] = silu(v).astype(jnp.bfloat16)
        for x in range(hi - lo):
            noise = conv_column(a2.at[s], w3_ref[...], x, hid, cin, first_o, last_o)[:nvars]
            current = ext[s, (x + 3) * cin : (x + 4) * cin, :].astype(jnp.float32)[:nvars]
            seen = obs_ref[lo + x].astype(jnp.float32)
            gain = 0.25 * ow_ref[lo + x]
            new = current - 0.5 * noise + gain * (seen - current)
            out_ref[0, at] = new.astype(jnp.bfloat16)
            at += 1


def update_chunk(spans, edges, mid, observed, obs_weight, w1, w2, w3, cin, hid):
    slots, _, nvars, lat = mid.shape
    step = sum(hi - lo for lo, hi in spans)
    widest = max(hi - lo for lo, hi in spans)
    whole = lambda a: pl.BlockSpec(a.shape, lambda p: (0,) * a.ndim)
    own = lambda a: pl.BlockSpec((1,) + a.shape[1:], lambda p: (p, 0, 0, 0))
    return pl.pallas_call(
        functools.partial(step_kernel, spans, cin, hid, bool(edges)),
        out_shape=jax.ShapeDtypeStruct((slots, step, nvars, lat), jnp.bfloat16),
        grid=(slots,),
        in_specs=[own(a) for a in (*edges, mid)]
        + [whole(a) for a in (observed, obs_weight, w1, w2, w3)],
        out_specs=pl.BlockSpec((1, step, nvars, lat), lambda p: (p, 0, 0, 0)),
        scratch_shapes=[
            pltpu.VMEM((len(spans), (widest + 6) * cin, lat), jnp.bfloat16),
            pltpu.VMEM((len(spans), (widest + 4) * hid, lat), jnp.bfloat16),
            pltpu.VMEM((len(spans), (widest + 2) * hid, lat), jnp.bfloat16),
        ],
        compiler_params=pltpu.CompilerParams(vmem_limit_bytes=56 << 20),
        cost_estimate=pl.CostEstimate(flops=0, bytes_accessed=1024, transcendentals=0),
        name="update_chunk",
    )(*edges, mid, observed, obs_weight, w1, w2, w3)


def exchange_kernel(n_lon, mid_ref, sums_ref, low_ref, high_ref, total_ref, parts, edge_send, edge_recv, lon_send, lon_recv):
    lon = lax.axis_index("lon")
    cols = mid_ref.shape[1]

    def lon_at(k):
        return {"lon": lax.rem(lon + k, n_lon)}

    barrier = pltpu.get_barrier_semaphore()
    for k in range(1, n_lon):
        pl.semaphore_signal(barrier, inc=1, device_id=lon_at(k), device_id_type=pl.DeviceIdType.MESH)
    pl.semaphore_wait(barrier, n_lon - 1)

    def send(src, dst, s, r, target):
        copy = pltpu.make_async_remote_copy(
            src_ref=src, dst_ref=dst, send_sem=s, recv_sem=r,
            device_id=target, device_id_type=pl.DeviceIdType.MESH,
        )
        copy.start()
        return copy

    edges = [
        send(mid_ref.at[:, cols - 3 : cols], low_ref, edge_send.at[0], edge_recv.at[0], lon_at(1)),
        send(mid_ref.at[:, 0:3], high_ref, edge_send.at[1], edge_recv.at[1], lon_at(n_lon - 1)),
    ]
    parts[lon] = sums_ref[...]
    over_lon = [
        send(sums_ref, parts.at[lon], lon_send.at[k - 1], lon_recv.at[k - 1], lon_at(k))
        for k in range(1, n_lon)
    ]
    for copy in over_lon:
        copy.wait()
    band_sum = parts[0]
    for k in range(1, n_lon):
        band_sum = band_sum + parts[k]
    total_ref[...] = band_sum
    for copy in edges:
        copy.wait()


def exchange(mid, sums, n_lon):
    slots, _, nvars, lat = mid.shape
    edge = jax.ShapeDtypeStruct((slots, 3, nvars, lat), mid.dtype)
    vmem = pl.BlockSpec(memory_space=pltpu.VMEM)
    return pl.pallas_call(
        functools.partial(exchange_kernel, n_lon),
        out_shape=(edge, edge, jax.ShapeDtypeStruct(sums.shape, jnp.float32)),
        in_specs=[pl.BlockSpec(memory_space=pl.ANY), vmem],
        out_specs=(vmem, vmem, vmem),
        scratch_shapes=[
            pltpu.VMEM((n_lon,) + sums.shape, jnp.float32),
            pltpu.SemaphoreType.DMA((2,)),
            pltpu.SemaphoreType.DMA((2,)),
            pltpu.SemaphoreType.DMA((n_lon - 1,)),
            pltpu.SemaphoreType.DMA((n_lon - 1,)),
        ],
        compiler_params=pltpu.CompilerParams(collective_id=0, has_side_effects=True),
        cost_estimate=pl.CostEstimate(flops=0, bytes_accessed=1024, transcendentals=0),
        name="exchange",
    )(mid, sums)


def across(u):
    n = lax.axis_size("dom")
    return [u] + [
        lax.ppermute(u, "dom", [(d, (d + 2 * k) % n) for d in range(n)]) for k in range(1, n // 2)
    ]


def pick_kernel(slots, base, codes_ref, *refs):
    *pieces, out_ref = refs
    if base == 0:
        received_ref, *pieces = pieces
    for s in range(slots):
        for m in range(len(pieces) * slots):
            wanted = codes_ref[base + s] == m
            if base == 0:
                wanted = wanted & (codes_ref[2 * slots + s] == 1)

            @pl.when(wanted)
            def _():
                out_ref[s] = pieces[m // slots][m % slots]

        if base == 0:

            @pl.when(codes_ref[2 * slots + s] == 0)
            def _():
                out_ref[s] = received_ref[s]


def pick(codes, base, arrays):
    u = arrays[0]
    slots = u.shape[0]
    vmem = pl.BlockSpec(memory_space=pltpu.VMEM)
    return pl.pallas_call(
        functools.partial(pick_kernel, slots, base),
        out_shape=jax.ShapeDtypeStruct(u.shape, u.dtype),
        in_specs=[pl.BlockSpec(memory_space=pltpu.SMEM)] + [vmem] * len(arrays),
        out_specs=vmem,
        compiler_params=pltpu.CompilerParams(vmem_limit_bytes=24 << 20),
        cost_estimate=pl.CostEstimate(flops=0, bytes_accessed=1024, transcendentals=0),
        name="pick",
    )(codes, *arrays)


def weight_kernel(slots, t_ref, *refs):
    *part_refs, out_ref = refs
    shape = out_ref.shape
    real = lax.broadcasted_iota(jnp.int32, shape, 0) < slots
    count = len(part_refs) * slots

    def over_particles(rows):
        total = rows[0]
        for row in rows[1:]:
            total = total + row
        return jnp.sum(total, axis=0, keepdims=True)

    misfits = [jnp.broadcast_to(jnp.sum(r[...], axis=1, keepdims=True), shape) for r in part_refs]
    center = over_particles([jnp.where(real, m, 0.0) for m in misfits]) / count
    deviations = [jnp.where(real, m - center, 0.0) for m in misfits]
    spread = jnp.sqrt(over_particles([d * d for d in deviations]) / count + 1.0)
    expos = [jnp.where(real, jnp.exp(-0.5 * t_ref[0] * d / spread), 0.0) for d in deviations]
    out_ref[...] = expos[0] / over_particles(expos)


def own_weights_of(parts, tempering, slots):
    vmem = pl.BlockSpec(memory_space=pltpu.VMEM)
    out = pl.pallas_call(
        functools.partial(weight_kernel, slots),
        out_shape=jax.ShapeDtypeStruct(parts[0].shape, jnp.float32),
        in_specs=[pl.BlockSpec(memory_space=pltpu.SMEM)] + [vmem] * len(parts),
        out_specs=vmem,
        name="own_weights",
    )(tempering, *parts)
    return out[:slots, 0]


def on_device(particles, observed, precision, stations, ancestors, tempering, w_in, w_mid, w_out):
    slots, nvars, cols, lat = particles.shape
    hid = w_mid.shape[2]
    cin = pad_to(nvars, 16)
    n_dom, n_lon = lax.axis_size("dom"), lax.axis_size("lon")
    me = lax.axis_index("dom")
    mid = particles.transpose(0, 2, 1, 3)
    sibling_anc = lax.ppermute(ancestors, "dom", [(d, d ^ 1) for d in range(n_dom)])

    obs_weight = stations.astype(jnp.float32) * precision
    wanted = jnp.concatenate([ancestors, sibling_anc])
    owner = lax.div(wanted, slots)
    chips = n_dom // 2
    steps = lax.rem(lax.shift_right_logical(me, 1) - lax.div(owner, 2) + chips, chips)
    candidate = steps * slots + lax.rem(wanted, slots)
    here = lax.rem(owner, 2) == (me & 1)

    obs_columns = observed.transpose(1, 0, 2)
    ow_columns = obs_weight[:, None, :]
    w1 = stacked_taps(w_in, hid, cin)
    w2 = stacked_taps(w_mid, hid, hid)
    w3 = stacked_taps(w_out, cin, hid)

    update = lambda spans, edges: update_chunk(
        spans, edges, mid, obs_columns, ow_columns, w1, w2, w3, cin, hid
    )
    u = update([(3, cols - 3)], [])
    groups = [across(u)]

    late_weight, _ = lax.optimization_barrier((obs_weight, u))
    misfit_cell = particles.astype(jnp.float32) - observed.astype(jnp.float32)[None]
    local_sums = jnp.sum(late_weight[None, None] * misfit_cell * misfit_cell, axis=(1, 2))
    sums = jnp.sum(local_sums.reshape(slots, lat // 128, 128), axis=1)
    sums = jnp.pad(sums, ((0, pad_to(slots, 8) - slots), (0, 0)))
    low, high, band_sums = exchange(mid, sums, n_lon)
    groups.append(across(update([(0, 3), (cols - 3, cols)], [low, high])))

    parts = [band_sums] + [
        lax.ppermute(band_sums, "dom", [(d, (d + k) % n_dom) for d in range(n_dom)])
        for k in range(1, n_dom)
    ]
    own_weights = own_weights_of(parts, tempering, slots)

    codes = jnp.concatenate([candidate, here[:slots].astype(jnp.int32)])
    groups = lax.optimization_barrier(groups)
    results = []
    for pieces in groups:
        sent = pick(codes, slots, pieces)
        received = lax.ppermute(sent, "dom", [(d, d ^ 1) for d in range(n_dom)])
        results.append(pick(codes, 0, [received, *pieces]))
    inner, sides = results
    new_columns = jnp.concatenate([sides[:, :3], inner, sides[:, 3:]], axis=1)
    return (new_columns.transpose(0, 2, 1, 3), own_weights)


def solution(mesh):
    return jax.shard_map(
        on_device,
        mesh=mesh,
        in_specs=(
            P(("ens", "dom"), None, "lon", None),
            P("ens", "lon", None),
            P(("ens", "lon"), None),
            P(("ens", "lon"), None),
            P(("ens", "dom")),
            P("ens"),
            P(),
            P(),
            P(),
        ),
        out_specs=(P(("ens", "dom"), None, "lon", None), P(("ens", "dom"))),
        check_vma=False,
    )
```
